32 devices in a mesh: row: 8 (over y, x, core), col: 4 (over z).
Axes of the slice: x: 2, y: 2, z: 4, core: 2. Of those that a mesh axis runs over, the one named last changes fastest.
Arguments:
- a_blocks: bfloat16 [256, 12, 4096], P('row', 'col'), may hold values from -0.75 to 0.75
- columns: int32 [256, 12], P('row', 'col'), may hold values from 0 to 255, as said below
- prolong: bfloat16 [256, 4096], P(('row', 'col')), may hold values from -1.5 to 1.5
- partner: int32 [256], P('row'), may hold values from 0 to 31, as said below
Outputs:
- coarse: bfloat16 [128, 12, 4096], P('row', 'col')
The draws below stay inside these ranges and needn't reach their ends.
Inputs may be any that keep to these rules, and one draw needn't show every extreme that they name: `columns`: entry k of a fine block row in row group g reaches a fine block row of group g - 1, g or g + 1 inside the grid, whose position within its group lies in [j * 8, (j + 1) * 8) with j = k // 3. Rows of groups 2q and 2q+1 are matched one to one: partner of a row in one group gives its partner's position in the other, and the two entries point at each other.
All inputs are finite; a program needn't handle non-finite values.
Results may differ from the reference program's by a relative error of at most 0.0058.
Values may be sent and summed in bfloat16 or wider, within the bound.
A program may use at most 64 MiB of HBM per device.

```python
import jax
import jax.numpy as jnp
from jax import lax

BS = 64
RD = 32
KD = 3
K = 12
RDC = 8
NB = 256


def draw_columns(key, part):
    groups = NB // RD
    first, second = jax.random.split(jax.random.fold_in(key, 11))
    row_ids = jnp.arange(NB, dtype=jnp.int32)[:, None]
    own_group = row_ids // RD
    offset = jax.random.randint(first, (NB, K), -1, 2, dtype=jnp.int32)
    target = jnp.clip(own_group + offset, 0, groups - 1)
    slot_group = jnp.arange(K, dtype=jnp.int32)[None, :] // KD
    within = slot_group * RDC + jax.random.randint(second, (NB, K), 0, RDC, dtype=jnp.int32)
    return (target * RD + within).astype(jnp.int32)


def draw_partner(key, part):
    pairs = NB // (2 * RD)
    keys = jax.random.split(jax.random.fold_in(key, 23), pairs)
    forward = jax.vmap(lambda one: jax.random.permutation(one, RD))(keys).astype(jnp.int32)
    backward = jnp.argsort(forward, axis=1, stable=True).astype(jnp.int32)
    return jnp.stack([forward, backward], axis=1).reshape(NB).astype(jnp.int32)


def levels(own_key, shape, cuts, smallest, top_value):
    loudness, own = 1.0, jax.random.fold_in(own_key, 6)
    for dim, blocks in cuts:
        steps = jnp.exp(jax.random.uniform(jax.random.fold_in(own, dim), (blocks,), jnp.float32, smallest / len(cuts), top_value / len(cuts)))
        loudness = loudness * jnp.repeat(steps, shape[dim] // blocks).reshape([-1 if axis == dim else 1 for axis in range(len(shape))])
    return loudness


def normal_values(rng, dims, scale, bound, cuts=(), held_as=jnp.bfloat16):
    drawn = scale * jax.random.normal(rng, dims, jnp.float32)
    if cuts:
        drawn = drawn * levels(rng, dims, cuts, -0.22, 0.18)
    return jnp.clip(drawn, -bound, bound).astype(held_as)


def setup_inputs(seed: int = 0) -> dict:
    key_of = jax.random.split(jax.random.key(seed), 5)
    return {
        "a_blocks": normal_values(key_of[0], (NB, K, BS * BS), 0.125, 0.75, ((0, 8), (1, 4))),
        "columns": draw_columns(jax.random.fold_in(key_of[4], 71), 0),
        "prolong": normal_values(key_of[2], (NB, BS * BS), 0.25, 1.5, ((0, 32),)),
        "partner": draw_partner(jax.random.fold_in(key_of[4], 71), 0),
    }


def reference(a_blocks, columns, prolong, partner):
    def one_pair(index):
        start = (index * 2 * RD).astype(jnp.int32)
        blocks = lax.dynamic_slice_in_dim(a_blocks, start, 2 * RD, 0).astype(jnp.float32).reshape(2 * RD, K, BS, BS)
        targets = lax.dynamic_slice_in_dim(columns, start, 2 * RD, 0)
        reached = jnp.take(prolong, targets, axis=0).astype(jnp.float32).reshape(2 * RD, K, BS, BS)
        product = jnp.einsum("rkab,rkbc->rkac", blocks, reached).astype(jnp.bfloat16)
        product = lax.optimization_barrier(product).astype(jnp.float32)
        own = lax.dynamic_slice_in_dim(prolong, start, 2 * RD, 0).astype(jnp.float32).reshape(2 * RD, BS, BS)
        term = jnp.einsum("rba,rkbc->rkac", own, product).astype(jnp.bfloat16)
        term = lax.optimization_barrier(term).astype(jnp.float32)
        matched = lax.dynamic_slice_in_dim(partner, start, RD, 0)
        total = term[:RD] + jnp.take(term[RD:], matched, axis=0)
        return total.astype(jnp.bfloat16).reshape(RD, K, BS * BS)

    result = lax.map(one_pair, jnp.arange(NB // (2 * RD), dtype=jnp.int32))
    return result.reshape(NB // 2, K, BS * BS)
```

```python
import functools
import math

import jax
import jax.numpy as jnp
from jax import lax
from jax.experimental import pallas as pl
from jax.experimental.pallas import tpu as pltpu
from jax.sharding import PartitionSpec as P

MESH = pl.DeviceIdType.MESH
BF = jnp.bfloat16
F32 = jnp.float32
LANES = 128


def iota(shape, dim):
    return lax.broadcasted_iota(jnp.int32, shape, dim)


def onehot(mask):
    return jnp.where(mask, 1.0, 0.0).astype(BF)


def kernel(dims, partner_hbm, cols_hbm, p_hbm, a_hbm, out_ref, partner_v, order_v, order, cols, p_ref, a_v, own_v, halo_v, af, hf, of, pf, bd, lv, wv, term_v, recv_v,
           partner_sem, order_sem, cols_sem, p_sem, a_sem, row_ready, col_ready, row_send, row_recv, col_send, col_recv, pair_send, pair_recv):
    nrow, ncol, rows, slots, thin, size, bs = dims
    tiles = size // LANES
    half = rows // 2
    g = lax.axis_index("row")
    z = lax.axis_index("col")
    odd = lax.rem(g, 2)
    pair = g + 1 - 2 * odd

    barrier = pltpu.get_barrier_semaphore()
    for d in range(ncol - 1, 0, -1):
        @pl.when(z + d < ncol)
        def _(d=d):
            pl.semaphore_signal(barrier, inc=1, device_id={"col": z + d}, device_id_type=MESH)

    @pl.when(g + 1 < nrow)
    def _():
        pl.semaphore_signal(barrier, inc=1, device_id={"row": g + 1}, device_id_type=MESH)

    local = pltpu.make_async_copy(p_hbm, p_ref, p_sem)
    local.start()
    partner_copy = pltpu.make_async_copy(partner_hbm, partner_v, partner_sem)
    partner_copy.start()
    cols_copy = pltpu.make_async_copy(cols_hbm, cols, cols_sem)
    cols_copy.start()
    fetch = pltpu.make_async_copy(a_hbm, a_v, a_sem)
    fetch.start()
    greeted = z + jnp.minimum(g, 1)

    @pl.when(greeted > 0)
    def _():
        pl.semaphore_wait(barrier, greeted)

    def col_copy(target, source):
        return pltpu.make_async_remote_copy(
            src_ref=p_hbm, dst_ref=own_v.at[source], send_sem=col_send.at[target], recv_sem=col_recv.at[source],
            device_id={"col": target}, device_id_type=MESH)

    def row_copy(target, slot):
        return pltpu.make_async_remote_copy(
            src_ref=p_hbm, dst_ref=halo_v.at[slot], send_sem=row_send.at[slot], recv_sem=row_recv.at[slot],
            device_id={"row": target}, device_id_type=MESH)

    def pair_copy(source):
        place = pl.ds(source * thin, thin)
        return pltpu.make_async_remote_copy(
            src_ref=term_v.at[place], dst_ref=recv_v.at[place],
            send_sem=pair_send.at[source], recv_sem=pair_recv.at[source], device_id={"row": pair}, device_id_type=MESH)

    def send_down(target):
        @pl.when(target < z)
        def _():
            col_copy(target, z).start()

    send_down(0)

    @pl.when(g > 0)
    def _():
        row_copy(g - 1, 1).start()
        pl.semaphore_signal(row_ready, inc=1, device_id={"row": g - 1}, device_id_type=MESH)

    for d in range(1, ncol):
        @pl.when(z >= d)
        def _(d=d):
            pl.semaphore_signal(col_ready.at[d], inc=1, device_id={"col": z - d}, device_id_type=MESH)

    def send_up(d):
        @pl.when(z + d < ncol)
        def _():
            pl.semaphore_wait(col_ready.at[d], 1)
            col_copy(z + d, z).start()

    def spread(source, target, base):
        for t in range(tiles):
            target[pl.ds(base + t * thin, thin), :] = source[:, t * LANES:(t + 1) * LANES].astype(F32)

    low = iota((tiles, LANES), 1) < bs
    r2, c2 = iota((2 * bs, 2 * bs), 0), iota((2 * bs, 2 * bs), 1)
    rh, ch = r2 // bs, c2 // bs
    rm, cm = r2 - rh * bs, c2 - ch * bs
    cs = cm // tiles
    weave = onehot((rh == ch) & (2 * (cm - cs * tiles) + cs == rm))
    r1, c1 = iota((bs, LANES), 0), iota((bs, LANES), 1)
    s1 = r1 // tiles
    pick = onehot(c1 == 2 * (r1 - s1 * tiles) + s1)

    def diagonals(slot):
        base = slot * tiles * thin
        for r in range(thin):
            packed = hf[pl.ds(base + r, tiles, stride=thin), :]
            turned = pltpu.roll(packed, bs, 1)
            zero = jnp.zeros_like(packed)
            stacked = jnp.concatenate(
                [jnp.where(low, packed, zero), jnp.where(low, turned, zero),
                 jnp.where(low, zero, turned), jnp.where(low, zero, packed)], axis=0).astype(BF)
            bd[slot * thin + r] = jnp.dot(weave, stacked, preferred_element_type=F32).astype(BF)

    local.wait()
    spread(p_ref, hf, tiles * thin)
    diagonals(1)
    for target in range(1, ncol - 1):
        @pl.when(z == ncol - 1)
        def _(target=target):
            send_down(target)

    partner_copy.wait()
    place = iota((rows, rows), 0)
    entry = iota((rows, rows), 1)
    held = jnp.broadcast_to(partner_v[...], (rows, rows))
    matched = jnp.where(odd == 1, jnp.where(held == place, entry, 0), jnp.where(entry == place, held, 0))
    picked = jnp.sum(matched.astype(F32), axis=1, keepdims=True)
    order_v[...] = jnp.broadcast_to(picked, (rows, LANES)).astype(jnp.int32)
    order_copy = pltpu.make_async_copy(order_v, order, order_sem)
    order_copy.start()

    @pl.when(g + 1 < nrow)
    def _():
        pl.semaphore_wait(row_ready, 1)
        row_copy(g + 1, 0).start()

    fetch.wait()
    for k in range(slots):
        def spread_a(h, _, k=k):
            top = pl.multiple_of(h * 16, 16)
            base = pl.multiple_of((k * rows + h * 16) * tiles, 8)
            for t in range(tiles):
                tile = a_v[k, pl.ds(top, 16), t * LANES:(t + 1) * LANES].astype(F32)
                af[pl.ds(base + t * 8, 8), :] = tile[:8]
                af[pl.ds(base + (tiles + t) * 8, 8), :] = tile[8:]
            return 0
        lax.fori_loop(0, rows // 16, spread_a, 0)

    send_up(1)

    def halo(slot):
        row_copy(pair, slot).wait_recv()
        spread(halo_v.at[slot], hf, 2 * slot * tiles * thin)
        diagonals(2 * slot)

    @pl.when(g + 1 < nrow)
    def _():
        halo(1)
    for target in range(1, ncol - 1):
        @pl.when(z < ncol - 1)
        def _(target=target):
            send_down(target)
    for d in range(2, ncol):
        send_up(d)

    @pl.when(g > 0)
    def _():
        halo(0)

    cols_copy.wait()
    shift = (1 - g) * thin - z * thin

    def product(ih, _):
        for il in range(8):
            i = ih * 8 + il
            for k in range(slots):
                c = cols[k, i]
                place = jnp.clip(c - lax.div(c, rows) * (rows - thin) + shift, 0, 3 * thin - 1)
                left = af[pl.ds(k * rows * tiles + ih * 8 * tiles + il, tiles, stride=8), :].astype(BF)
                prod = jnp.dot(left, bd[place], preferred_element_type=F32)
                wv[i, :, k * LANES:(k + 1) * LANES] = jnp.concatenate(
                    [prod, pltpu.roll(prod, bs, 1)], axis=0).astype(BF)
        return 0
    lax.fori_loop(0, rows // 8, product, 0)

    def lefts(source, j):
        spread(source, pf, 0)
        for r in range(thin):
            packed = pf[pl.ds(r, tiles, stride=thin), :]
            stacked = jnp.concatenate([packed, pltpu.roll(packed, bs, 1)], axis=0).astype(BF)
            lv[j * thin + r] = lax.dot_general(
                pick, stacked, (((1,), (1,)), ((), ())), preferred_element_type=F32).astype(BF)

    def terms(source, j):
        lefts(source, j)
        for r in range(thin):
            i = j * thin + r
            full = jnp.dot(lv[i], wv[i], preferred_element_type=F32)
            for k in range(slots):
                part = full[:, k * LANES:(k + 1) * LANES]
                term_v[i, k] = jnp.where(low, part[:tiles], pltpu.roll(part[tiles:], bs, 1)).astype(BF)

        @pl.when((odd == 1) | (2 * j >= ncol))
        def _():
            pair_copy(j).start()

    inner = jnp.minimum(z, ncol - 1 - z)
    terms(p_ref, z)
    for s in range(1, ncol):
        near = z - (s + 1) // 2 if s % 2 else z + s // 2
        j = jnp.where(s <= 2 * inner, near, jnp.where(2 * z < ncol - 1, s, ncol - 1 - s))
        col_copy(j, j).wait_recv()
        terms(own_v.at[j], j)

    order_copy.wait()
    for j in range(ncol):
        @pl.when((odd == 0) | (2 * j >= ncol))
        def _(j=j):
            pair_copy(j).wait_recv()
    for j in range(half):
        found = jnp.clip(order[odd * half + j, 0], 0, rows - 1)
        mine = jnp.where(odd == 1, found, j)
        other = jnp.where(odd == 1, half + j, found)
        for k in range(slots):
            total = term_v[mine, k].astype(F32) + recv_v[other, k].astype(F32)
            of[pl.ds((k * half + j // 8 * 8) * tiles + j % 8, tiles, stride=8), :] = total
    for k in range(slots):
        for h in range(half // 16):
            base = (k * half + h * 16) * tiles
            for t in range(tiles):
                tile = jnp.concatenate(
                    [of[pl.ds(base + t * 8, 8), :], of[pl.ds(base + (tiles + t) * 8, 8), :]], axis=0)
                out_ref[k, h * 16:(h + 1) * 16, t * LANES:(t + 1) * LANES] = tile.astype(BF)

    for j in range(ncol):
        @pl.when((odd == 1) | (2 * j >= ncol))
        def _(j=j):
            pair_copy(j).wait_send()

        @pl.when(j != z)
        def _(j=j):
            col_copy(j, z).wait_send()
    for slot in range(2):
        @pl.when((g > 0) if slot else (g + 1 < nrow))
        def _(slot=slot):
            row_copy(pair, slot).wait_send()


def on_device(nrow, ncol, a_blocks, columns, prolong, partner):
    rows, slots, size = a_blocks.shape
    thin = prolong.shape[0]
    bs = math.isqrt(size)
    tiles = size // LANES
    half = rows // 2
    dims = (nrow, ncol, rows, slots, thin, size, bs)
    hbm = pl.BlockSpec(memory_space=pltpu.HBM)
    vmem = pl.BlockSpec(memory_space=pltpu.VMEM)
    out = pl.pallas_call(
        functools.partial(kernel, dims),
        out_shape=pltpu.VMEM((slots, half, size), BF),
        in_specs=[hbm] * 4,
        out_specs=vmem,
        scratch_shapes=[
            pltpu.VMEM((1, rows), jnp.int32),
            pltpu.VMEM((rows, LANES), jnp.int32),
            pltpu.SMEM((rows, LANES), jnp.int32),
            pltpu.SMEM((slots, rows), jnp.int32),
            pltpu.VMEM((thin, size), BF),
            pltpu.VMEM((slots, rows, size), BF),
            pltpu.VMEM((ncol, thin, size), BF),
            pltpu.VMEM((2, thin, size), BF),
            pltpu.VMEM((slots * rows * tiles, LANES), F32),
            pltpu.VMEM((3 * tiles * thin, LANES), F32),
            pltpu.VMEM((slots * half * tiles, LANES), F32),
            pltpu.VMEM((tiles * thin, LANES), F32),
            pltpu.VMEM((3 * thin, LANES, LANES), BF),
            pltpu.VMEM((rows, bs, bs), BF),
            pltpu.VMEM((rows, bs, slots * LANES), BF),
            pltpu.VMEM((rows, slots, tiles, LANES), BF),
            pltpu.VMEM((rows, slots, tiles, LANES), BF),
            pltpu.SemaphoreType.DMA,
            pltpu.SemaphoreType.DMA,
            pltpu.SemaphoreType.DMA,
            pltpu.SemaphoreType.DMA,
            pltpu.SemaphoreType.DMA,
            pltpu.SemaphoreType.REGULAR,
            pltpu.SemaphoreType.REGULAR((ncol,)),
            pltpu.SemaphoreType.DMA((2,)),
            pltpu.SemaphoreType.DMA((2,)),
            pltpu.SemaphoreType.DMA((ncol,)),
            pltpu.SemaphoreType.DMA((ncol,)),
            pltpu.SemaphoreType.DMA((ncol,)),
            pltpu.SemaphoreType.DMA((ncol,)),
        ],
        compiler_params=pltpu.CompilerParams(
            collective_id=0, has_side_effects=True, vmem_limit_bytes=32 * 2**20),
    )(*(pltpu.with_memory_space_constraint(x, pltpu.HBM) for x in (partner.reshape(1, rows), columns.T, prolong, a_blocks.transpose(1, 0, 2))))
    return out.transpose(1, 0, 2)


def solution(mesh):
    in_specs = (P("row", "col", None), P("row", "col"), P(("row", "col"), None), P("row"))
    out_specs = P("row", "col", None)
    return jax.shard_map(
        functools.partial(on_device, mesh.shape["row"], mesh.shape["col"]),
        mesh=mesh, in_specs=in_specs, out_specs=out_specs, check_vma=False
    )
```

```python
import functools
import math

import jax
import jax.numpy as jnp
from jax import lax
from jax.experimental import pallas as pl
from jax.experimental.pallas import tpu as pltpu
from jax.sharding import PartitionSpec as P

MESH = pl.DeviceIdType.MESH
BF = jnp.bfloat16
F32 = jnp.float32
LANES = 128


def iota(shape, dim):
    return lax.broadcasted_iota(jnp.int32, shape, dim)


def onehot(mask):
    return jnp.where(mask, 1.0, 0.0).astype(BF)


def kernel(dims, partner_hbm, cols_hbm, p_hbm, a_hbm, out_ref, partner_v, order_v, order, cols, p_ref, a_v, own_v, halo_v, af, hf, of, pf, bd, lv, wv, term_v, recv_v,
           partner_sem, order_sem, cols_sem, p_sem, a_sem, row_ready, col_ready, row_send, row_recv, col_send, col_recv, pair_send, pair_recv):
    nrow, ncol, rows, slots, thin, size, bs = dims
    tiles = size // LANES
    half = rows // 2
    g = lax.axis_index("row")
    z = lax.axis_index("col")
    odd = lax.rem(g, 2)
    pair = g + 1 - 2 * odd

    barrier = pltpu.get_barrier_semaphore()
    for d in range(ncol - 1, 0, -1):
        @pl.when(z + d < ncol)
        def _(d=d):
            pl.semaphore_signal(barrier, inc=1, device_id={"col": z + d}, device_id_type=MESH)

    @pl.when(g + 1 < nrow)
    def _():
        pl.semaphore_signal(barrier, inc=1, device_id={"row": g + 1}, device_id_type=MESH)

    local = pltpu.make_async_copy(p_hbm, p_ref, p_sem)
    local.start()
    partner_copy = pltpu.make_async_copy(partner_hbm, partner_v, partner_sem)
    partner_copy.start()
    cols_copy = pltpu.make_async_copy(cols_hbm, cols, cols_sem)
    cols_copy.start()
    fetch = pltpu.make_async_copy(a_hbm, a_v, a_sem)
    fetch.start()
    greeted = z + jnp.minimum(g, 1)

    @pl.when(greeted > 0)
    def _():
        pl.semaphore_wait(barrier, greeted)

    def col_copy(target, source):
        return pltpu.make_async_remote_copy(
            src_ref=p_hbm, dst_ref=own_v.at[source], send_sem=col_send.at[target], recv_sem=col_recv.at[source],
            device_id={"col": target}, device_id_type=MESH)

    def row_copy(target, slot):
        return pltpu.make_async_remote_copy(
            src_ref=p_hbm, dst_ref=halo_v.at[slot], send_sem=row_send.at[slot], recv_sem=row_recv.at[slot],
            device_id={"row": target}, device_id_type=MESH)

    def pair_copy(source):
        place = pl.ds(source * thin, thin)
        return pltpu.make_async_remote_copy(
            src_ref=term_v.at[place], dst_ref=recv_v.at[place],
            send_sem=pair_send.at[source], recv_sem=pair_recv.at[source], device_id={"row": pair}, device_id_type=MESH)

    def send_down(target):
        @pl.when(target < z)
        def _():
            col_copy(target, z).start()

    send_down(0)

    @pl.when(g > 0)
    def _():
        row_copy(g - 1, 1).start()
        pl.semaphore_signal(row_ready, inc=1, device_id={"row": g - 1}, device_id_type=MESH)

    for d in range(1, ncol):
        @pl.when(z >= d)
        def _(d=d):
            pl.semaphore_signal(col_ready.at[d], inc=1, device_id={"col": z - d}, device_id_type=MESH)

    def send_up(d):
        @pl.when(z + d < ncol)
        def _():
            pl.semaphore_wait(col_ready.at[d], 1)
            col_copy(z + d, z).start()

    def spread(source, target, base):
        for t in range(tiles):
            target[pl.ds(base + t * thin, thin), :] = source[:, t * LANES:(t + 1) * LANES].astype(F32)

    low = iota((tiles, LANES), 1) < bs
    r2, c2 = iota((2 * bs, 2 * bs), 0), iota((2 * bs, 2 * bs), 1)
    rh, ch = r2 // bs, c2 // bs
    rm, cm = r2 - rh * bs, c2 - ch * bs
    cs = cm // tiles
    weave = onehot((rh == ch) & (2 * (cm - cs * tiles) + cs == rm))
    r1, c1 = iota((bs, LANES), 0), iota((bs, LANES), 1)
    s1 = r1 // tiles
    pick = onehot(c1 == 2 * (r1 - s1 * tiles) + s1 * (bs + 1))

    def diagonals(slot):
        base = slot * tiles * thin
        for r in range(thin):
            packed = hf[pl.ds(base + r, tiles, stride=thin), :]
            turned = pltpu.roll(packed, bs, 1)
            zero = jnp.zeros_like(packed)
            stacked = jnp.concatenate(
                [jnp.where(low, packed, zero), jnp.where(low, turned, zero),
                 jnp.where(low, zero, turned), jnp.where(low, zero, packed)], axis=0).astype(BF)
            bd[slot * thin + r] = jnp.dot(weave, stacked, preferred_element_type=F32).astype(BF)

    local.wait()
    spread(p_ref, hf, tiles * thin)
    diagonals(1)

    partner_copy.wait()
    place = iota((rows, rows), 0)
    entry = iota((rows, rows), 1)
    held = jnp.broadcast_to(partner_v[...], (rows, rows))
    matched = jnp.where(odd == 1, jnp.where(held == place, entry, 0), jnp.where(entry == place, held, 0))
    picked = jnp.sum(matched.astype(F32), axis=1, keepdims=True)
    order_v[...] = jnp.broadcast_to(picked, (rows, LANES)).astype(jnp.int32)
    order_copy = pltpu.make_async_copy(order_v, order, order_sem)
    order_copy.start()

    def greet_row(side):
        @pl.when((g + 1 < nrow) & (odd == side))
        def _():
            pl.semaphore_wait(row_ready, 1)
            row_copy(g + 1, 0).start()

    greet_row(0)
    fetch.wait()
    for k in range(slots):
        def spread_a(h, _, k=k):
            top = pl.multiple_of(h * 16, 16)
            base = pl.multiple_of((k * rows + h * 16) * tiles, 8)
            for t in range(tiles):
                tile = a_v[k, pl.ds(top, 16), t * LANES:(t + 1) * LANES].astype(F32)
                af[pl.ds(base + t * 8, 8), :] = tile[:8]
                af[pl.ds(base + (tiles + t) * 8, 8), :] = tile[8:]
            return 0
        lax.fori_loop(0, rows // 16, spread_a, 0)

    send_up(1)
    greet_row(1)
    for d in range(2, ncol):
        send_up(d)

    def halo(slot):
        row_copy(pair, slot).wait_recv()
        spread(halo_v.at[slot], hf, 2 * slot * tiles * thin)
        diagonals(2 * slot)

    @pl.when(g + 1 < nrow)
    def _():
        halo(1)
    for target in range(1, ncol - 1):
        send_down(target)

    @pl.when(g > 0)
    def _():
        halo(0)

    cols_copy.wait()
    shift = (1 - g) * thin - z * thin

    def product(ih, _):
        for il in range(8):
            i = ih * 8 + il
            for k in range(slots):
                c = cols[k, i]
                place = jnp.clip(c - lax.div(c, rows) * (rows - thin) + shift, 0, 3 * thin - 1)
                left = af[pl.ds(k * rows * tiles + ih * 8 * tiles + il, tiles, stride=8), :].astype(BF)
                prod = jnp.dot(left, bd[place], preferred_element_type=F32)
                wv[i, :, k * LANES:(k + 1) * LANES] = jnp.concatenate(
                    [prod, pltpu.roll(prod, bs, 1)], axis=0).astype(BF)
        return 0
    lax.fori_loop(0, rows // 8, product, 0)

    def lefts(source, j):
        spread(source, pf, 0)
        for r in range(thin):
            packed = pf[pl.ds(r, tiles, stride=thin), :]
            stacked = jnp.concatenate([packed, pltpu.roll(packed, bs, 1)], axis=0).astype(BF)
            lv[j * thin + r] = lax.dot_general(
                pick, stacked, (((1,), (1,)), ((), ())), preferred_element_type=F32).astype(BF)

    def terms(source, j):
        lefts(source, j)
        for r in range(thin):
            i = j * thin + r
            full = jnp.dot(lv[i], wv[i], preferred_element_type=F32)
            for k in range(slots):
                part = full[:, k * LANES:(k + 1) * LANES]
                term_v[i, k] = jnp.where(low, part[:tiles], part[tiles:]).astype(BF)

        @pl.when((odd == 1) | (2 * j >= ncol))
        def _():
            pair_copy(j).start()

    inner = jnp.minimum(z, ncol - 1 - z)
    terms(p_ref, z)
    for s in range(1, ncol):
        near = z - (s + 1) // 2 if s % 2 else z + s // 2
        j = jnp.where(s <= 2 * inner, near, jnp.where(2 * z < ncol - 1, s, ncol - 1 - s))
        col_copy(j, j).wait_recv()
        terms(own_v.at[j], j)

    order_copy.wait()
    for j in range(ncol):
        @pl.when((odd == 0) | (2 * j >= ncol))
        def _(j=j):
            pair_copy(j).wait_recv()
    for j in range(half):
        found = jnp.clip(order[odd * half + j, 0], 0, rows - 1)
        mine = jnp.where(odd == 1, found, j)
        other = jnp.where(odd == 1, half + j, found)
        for k in range(slots):
            total = term_v[mine, k].astype(F32) + recv_v[other, k].astype(F32)
            of[pl.ds((k * half + j // 8 * 8) * tiles + j % 8, tiles, stride=8), :] = total
    for k in range(slots):
        for h in range(half // 16):
            base = (k * half + h * 16) * tiles
            for t in range(tiles):
                tile = jnp.concatenate(
                    [of[pl.ds(base + t * 8, 8), :], of[pl.ds(base + (tiles + t) * 8, 8), :]], axis=0)
                out_ref[k, h * 16:(h + 1) * 16, t * LANES:(t + 1) * LANES] = tile.astype(BF)

    for j in range(ncol):
        @pl.when((odd == 1) | (2 * j >= ncol))
        def _(j=j):
            pair_copy(j).wait_send()

        @pl.when(j != z)
        def _(j=j):
            col_copy(j, z).wait_send()
    for slot in range(2):
        @pl.when((g > 0) if slot else (g + 1 < nrow))
        def _(slot=slot):
            row_copy(pair, slot).wait_send()


def on_device(nrow, ncol, a_blocks, columns, prolong, partner):
    rows, slots, size = a_blocks.shape
    thin = prolong.shape[0]
    bs = math.isqrt(size)
    tiles = size // LANES
    half = rows // 2
    dims = (nrow, ncol, rows, slots, thin, size, bs)
    hbm = pl.BlockSpec(memory_space=pltpu.HBM)
    vmem = pl.BlockSpec(memory_space=pltpu.VMEM)
    out = pl.pallas_call(
        functools.partial(kernel, dims),
        out_shape=pltpu.VMEM((slots, half, size), BF),
        in_specs=[hbm] * 4,
        out_specs=vmem,
        scratch_shapes=[
            pltpu.VMEM((1, rows), jnp.int32),
            pltpu.VMEM((rows, LANES), jnp.int32),
            pltpu.SMEM((rows, LANES), jnp.int32),
            pltpu.SMEM((slots, rows), jnp.int32),
            pltpu.VMEM((thin, size), BF),
            pltpu.VMEM((slots, rows, size), BF),
            pltpu.VMEM((ncol, thin, size), BF),
            pltpu.VMEM((2, thin, size), BF),
            pltpu.VMEM((slots * rows * tiles, LANES), F32),
            pltpu.VMEM((3 * tiles * thin, LANES), F32),
            pltpu.VMEM((slots * half * tiles, LANES), F32),
            pltpu.VMEM((tiles * thin, LANES), F32),
            pltpu.VMEM((3 * thin, LANES, LANES), BF),
            pltpu.VMEM((rows, bs, bs), BF),
            pltpu.VMEM((rows, bs, slots * LANES), BF),
            pltpu.VMEM((rows, slots, tiles, LANES), BF),
            pltpu.VMEM((rows, slots, tiles, LANES), BF),
            pltpu.SemaphoreType.DMA,
            pltpu.SemaphoreType.DMA,
            pltpu.SemaphoreType.DMA,
            pltpu.SemaphoreType.DMA,
            pltpu.SemaphoreType.DMA,
            pltpu.SemaphoreType.REGULAR,
            pltpu.SemaphoreType.REGULAR((ncol,)),
            pltpu.SemaphoreType.DMA((2,)),
            pltpu.SemaphoreType.DMA((2,)),
            pltpu.SemaphoreType.DMA((ncol,)),
            pltpu.SemaphoreType.DMA((ncol,)),
            pltpu.SemaphoreType.DMA((ncol,)),
            pltpu.SemaphoreType.DMA((ncol,)),
        ],
        compiler_params=pltpu.CompilerParams(
            collective_id=0, has_side_effects=True, vmem_limit_bytes=32 * 2**20),
    )(*(pltpu.with_memory_space_constraint(x, pltpu.HBM) for x in (partner.reshape(1, rows), columns.T, prolong, a_blocks.transpose(1, 0, 2))))
    return out.transpose(1, 0, 2)


def solution(mesh):
    in_specs = (P("row", "col", None), P("row", "col"), P(("row", "col"), None), P("row"))
    out_specs = P("row", "col", None)
    return jax.shard_map(
        functools.partial(on_device, mesh.shape["row"], mesh.shape["col"]),
        mesh=mesh, in_specs=in_specs, out_specs=out_specs, check_vma=False
    )
```
